32 devices in a mesh: kv: 4 (over y, x), req: 8 (over z, core).
Axes of the slice: x: 2, y: 2, z: 4, core: 2. Of those that a mesh axis runs over, the one named last changes fastest.
Arguments:
- hidden: bfloat16 [64, 8192], P('kv', 'req'), may hold values from -6 to 6
- norm_gain: bfloat16 [8192], P('req'), may hold values from 0.5 to 1.5
- query_key_value_matrix: bfloat16 [8192, 8, 10, 128], P('req', 'kv'), may hold values from -1 to 1
- output_matrix: bfloat16 [8, 8, 128, 8192], P('kv', None, None, 'req'), may hold values from -3 to 3
- prefix_cache: bfloat16 [2, 256, 128, 2, 8, 128], P(None, 'req', None, None, 'kv'), may hold values from -60 to 60
- tail_cache: bfloat16 [2, 64, 64, 2, 8, 128], P(None, 'req', None, None, 'kv'), may hold values from -60 to 60
- prefix_group: int32 [64], P('req'), may hold values from 0 to 1
- prefix_len: int32 [16], P('req'), may hold values from 1 to 2048, 16384 in all
- prefix_pages: int32 [16, 16], P('req'), may hold values from 0 to 31, as said below
- tail_len: int32 [64], P('req'), may hold values from 1 to 64, 2048 in all
Outputs:
- next_hidden: bfloat16 [64, 8192], P('kv', 'req')
The draws below stay inside these ranges and needn't reach their ends.
Inputs may be any that keep to these rules, and one draw needn't show every extreme that they name: `prefix_pages`: within the 2 rows of one block of groups, the page numbers are a permutation of 0 to 31 and number the pages of that block.
All inputs are finite; a program needn't handle non-finite values. No bound on the sum of `prefix_len` or of `tail_len` on one device may be relied on, other than what follows from the above.
Results may differ from the reference program's by a relative error of at most 0.014.
The reference program's roundings to bfloat16 on the way count: a program that leaves them out, or rounds other values in their place, can miss the bound.
Values may be sent and summed in bfloat16 or wider, within the bound.
A program may use at most 192 MiB of HBM per device.

```python
import math
import jax
import jax.numpy as jnp
import numpy as np
from jax import lax

MODEL_WIDTH = 8192
QUERY_HEADS = 64
KEY_VALUE_HEADS = 8
HEAD_DIMENSION = 128
REQ_DEV = 8
GROUPS_DEV = 2
PAGE_TOKENS = 128
PREFIX_PAGE_COUNT = 16
TAIL_TOKENS = 64
LAYER_REPEATS = 2
REQUEST_COUNT = 64
PROMPT_GROUPS = 16
PREFIX_TOKENS = 2048


def cached_value_rows(key, full_shape):
    values = jax.random.normal(key, full_shape, jnp.float32)
    factor = jnp.array([2.0, 1.0], jnp.float32).reshape((2, 1, 1))
    offset = jnp.array([0.0, 0.5], jnp.float32).reshape((2, 1, 1))
    return jnp.clip(values * factor + offset, -60.0, 60.0).astype(jnp.bfloat16)


def draw_prefix_cache(key, part):
    return cached_value_rows(jax.random.fold_in(key, 11), (LAYER_REPEATS, PROMPT_GROUPS * PREFIX_PAGE_COUNT, PAGE_TOKENS, 2, KEY_VALUE_HEADS, HEAD_DIMENSION))


def draw_tail_cache(key, part):
    return cached_value_rows(jax.random.fold_in(key, 13), (LAYER_REPEATS, REQUEST_COUNT, TAIL_TOKENS, 2, KEY_VALUE_HEADS, HEAD_DIMENSION))


def draw_prefix_pages(key, part):
    blocks = PROMPT_GROUPS // GROUPS_DEV
    block_keys = jax.random.split(jax.random.fold_in(key, 17), blocks)
    orders = jax.vmap(lambda block_key: jax.random.permutation(block_key, GROUPS_DEV * PREFIX_PAGE_COUNT))(block_keys)
    return orders.reshape(PROMPT_GROUPS, PREFIX_PAGE_COUNT).astype(jnp.int32)


def unit_entries(key, full_shape):
    return jnp.clip(jax.random.normal(key, full_shape, jnp.float32), -6.0, 6.0)


def draw_query_key_value_matrix(key, part):
    per_head = QUERY_HEADS // KEY_VALUE_HEADS
    full_shape = (MODEL_WIDTH, KEY_VALUE_HEADS, per_head + 2, HEAD_DIMENSION)
    entries = unit_entries(jax.random.fold_in(key, 21), full_shape)
    chosen = jax.random.randint(jax.random.fold_in(key, 23), (KEY_VALUE_HEADS,), 0, per_head).astype(jnp.int32)
    picked = jnp.take_along_axis(entries[:, :, :per_head], chosen[None, :, None, None], axis=2)[:, :, 0]
    mixed_key = 0.8 * picked + 0.6 * entries[:, :, per_head]
    entries = entries.at[:, :, per_head].set(mixed_key)
    spread = MODEL_WIDTH ** (-0.5)
    return jnp.clip(entries * spread, -1.0, 1.0).astype(jnp.bfloat16)


def draw_output_matrix(key, part):
    per_head = QUERY_HEADS // KEY_VALUE_HEADS
    full_shape = (KEY_VALUE_HEADS, per_head, HEAD_DIMENSION, MODEL_WIDTH)
    entries = unit_entries(jax.random.fold_in(key, 27), full_shape)
    spread = (QUERY_HEADS * HEAD_DIMENSION // 16) ** (-0.5)
    column_offset = jnp.clip(jax.random.normal(jax.random.fold_in(key, 29), (MODEL_WIDTH,), jnp.float32), -4.0, 4.0)
    column_offset = column_offset * (1.6 / (QUERY_HEADS * HEAD_DIMENSION))
    return jnp.clip(entries * spread + column_offset, -3.0, 3.0).astype(jnp.bfloat16)


def touch_ends(drawn, rng, low, largest):
    dims = drawn.shape
    spot = [jax.random.randint(jax.random.fold_in(rng, axis), (), 0, dims[axis]) for axis in range(len(dims))]
    drawn = drawn.at[tuple(spot)].set(low)
    longest = dims.index(max(dims))
    spot[longest] = (spot[longest] + 1) % dims[longest]
    return drawn.at[tuple(spot)].set(largest)


def steps_of(key, dims, shards, smallest, largest):
    loudness, own = 1.0, jax.random.fold_in(key, 6)
    for axis_at, shards_of in shards:
        steps = jnp.exp(jax.random.uniform(jax.random.fold_in(own, axis_at), (shards_of,), jnp.float32, smallest / len(shards), largest / len(shards)))
        loudness = loudness * jnp.repeat(steps, dims[axis_at] // shards_of).reshape([-1 if axis == axis_at else 1 for axis in range(len(dims))])
    return loudness


def split_up(count, total, bound, lean):
    portions = [(1 << 20) // math.isqrt(standing ** lean) + 1 for standing in range(2, count + 1)]
    rest, counts = total - bound - (count - 1), [1] * (count - 1)
    while rest > 0:
        movable = [i for i in range(count - 1) if counts[i] < bound]
        whole, remaining = sum([portions[i] for i in movable]), rest
        for i in movable:
            more = min(bound - counts[i], max(1, remaining * portions[i] // whole), rest)
            counts[i] = counts[i] + more
            rest = rest - more
    return np.array([bound] + counts)


def ragged(rng, amount, total, bound, lean):
    if amount == 2:
        one = jax.random.randint(rng, (), max(1, total - bound), min(bound, total - 1) + 1)
        return jnp.stack([one, total - one])
    tallies = jnp.asarray(split_up(amount, total, bound, lean), jnp.int32)
    twos = (amount - 1) // 2
    donor, sink = tallies[1:1 + 2 * twos:2], tallies[2:2 + 2 * twos:2]
    margin = jnp.minimum(donor - 1, bound - sink)
    shifted = jax.random.randint(jax.random.fold_in(rng, 1), (twos,), 0, 1 << 20) % (margin + 1)
    tallies = tallies.at[1:1 + 2 * twos:2].set(donor - shifted).at[2:2 + 2 * twos:2].set(sink + shifted)
    return tallies[jax.random.permutation(jax.random.fold_in(rng, 2), amount)]


def normal_values(key, dims, scale, bound, pieces=(), kind=jnp.bfloat16):
    values = jax.random.normal(key, dims, jnp.float32) * scale
    if len(pieces) > 0:
        values = steps_of(key, dims, pieces, -0.22, 0.18) * values
    return jnp.clip(values, min=-bound, max=bound).astype(kind)


def setup_inputs(seed: int = 0) -> dict:
    arg_keys = jax.random.split(jax.random.key(seed), 11)
    return {
        "hidden": normal_values(arg_keys[0], (REQUEST_COUNT, MODEL_WIDTH), 1.0, 6.0, ((0, 4), (1, 8))),
        "norm_gain": jnp.clip(1.0 + 0.1 * jax.random.normal(arg_keys[1], (MODEL_WIDTH,), jnp.float32), 0.5, 1.5).astype(jnp.bfloat16),
        "query_key_value_matrix": draw_query_key_value_matrix(jax.random.fold_in(arg_keys[10], 71), 0),
        "output_matrix": draw_output_matrix(jax.random.fold_in(arg_keys[10], 71), 0),
        "prefix_cache": draw_prefix_cache(jax.random.fold_in(arg_keys[10], 71), 0),
        "tail_cache": draw_tail_cache(jax.random.fold_in(arg_keys[10], 71), 0),
        "prefix_group": touch_ends(jax.random.randint(arg_keys[6], (REQUEST_COUNT,), 0, GROUPS_DEV), jax.random.fold_in(arg_keys[6], 1), 0, GROUPS_DEV - 1).astype(jnp.int32),
        "prefix_len": ragged(arg_keys[7], PROMPT_GROUPS, PROMPT_GROUPS * PREFIX_TOKENS // 2, PREFIX_TOKENS, 1).astype(jnp.int32),
        "prefix_pages": draw_prefix_pages(jax.random.fold_in(arg_keys[10], 71), 0),
        "tail_len": ragged(arg_keys[9], REQUEST_COUNT, REQUEST_COUNT * TAIL_TOKENS // 2, TAIL_TOKENS, 1).astype(jnp.int32),
    }


def attend_one(queries, key_rows, value_rows, is_valid):
    scores = jnp.einsum('cqd,ncd->cqn', queries.astype(jnp.float32), key_rows.astype(jnp.float32)) * HEAD_DIMENSION ** (-0.5)
    scores = jnp.where(is_valid[None, None, :], scores, -1e+30)
    row_max = lax.optimization_barrier(jnp.max(scores, axis=-1, keepdims=True))
    weights = jnp.where(is_valid[None, None, :], jnp.exp(scores - row_max), 0.0)
    denominator = lax.optimization_barrier(jnp.sum(weights, axis=-1, keepdims=True))
    rounded = lax.optimization_barrier(weights.astype(jnp.bfloat16)).astype(jnp.float32)
    mixed = jnp.einsum('cqn,ncd->cqd', rounded, value_rows.astype(jnp.float32))
    return (mixed / denominator).astype(jnp.bfloat16)

def reference(hidden, norm_gain, query_key_value_matrix, output_matrix, prefix_cache, tail_cache, prefix_group, prefix_len, prefix_pages, tail_len):
    query_group_width = QUERY_HEADS // KEY_VALUE_HEADS
    flattened_weight = query_key_value_matrix.reshape(MODEL_WIDTH, KEY_VALUE_HEADS * (query_group_width + 2) * HEAD_DIMENSION)
    weight_out = output_matrix.reshape(QUERY_HEADS * HEAD_DIMENSION, MODEL_WIDTH)
    request_ids = jnp.arange(REQUEST_COUNT, dtype=jnp.int32)
    owner = request_ids // REQ_DEV
    group_ids = (owner * GROUPS_DEV + prefix_group).astype(jnp.int32)
    page_rows = (prefix_pages[group_ids] + (owner * (GROUPS_DEV * PREFIX_PAGE_COUNT))[:, None]).astype(jnp.int32)
    prefix_counts = prefix_len[group_ids]
    gain_f32 = norm_gain.astype(jnp.float32)
    state = hidden
    for layer_index in range(LAYER_REPEATS):
        state_f32 = state.astype(jnp.float32)
        mean_sq = lax.optimization_barrier(jnp.mean(state_f32 * state_f32, axis=1, keepdims=True))
        normed = (state_f32 * lax.rsqrt(mean_sq + 1e-05) * gain_f32[None, :]).astype(jnp.bfloat16)
        projected_rows = jnp.dot(normed, flattened_weight, preferred_element_type=jnp.float32).astype(jnp.bfloat16)
        projected_rows = projected_rows.reshape(REQUEST_COUNT, KEY_VALUE_HEADS, query_group_width + 2, HEAD_DIMENSION)
        shared_prefix_store = prefix_cache[layer_index]
        tail_pool = tail_cache[layer_index]

        def per_request(items):
            queries, key_new, value_new, page_row_entries, prefix_count, tail_rows, tail_count = items
            page_contents = jnp.take(shared_prefix_store, page_row_entries, axis=0).reshape(PREFIX_TOKENS, 2, KEY_VALUE_HEADS, HEAD_DIMENSION)
            key_rows = jnp.concatenate([page_contents[:, 0], tail_rows[:, 0], key_new[None]], axis=0)
            value_rows = jnp.concatenate([page_contents[:, 1], tail_rows[:, 1], value_new[None]], axis=0)
            is_valid = jnp.concatenate([jnp.arange(PREFIX_TOKENS, dtype=jnp.int32) < prefix_count, jnp.arange(TAIL_TOKENS, dtype=jnp.int32) < tail_count, jnp.ones((1,), dtype=bool)])
            return attend_one(queries, key_rows, value_rows, is_valid)
        attended = lax.map(per_request, (projected_rows[:, :, :query_group_width], projected_rows[:, :, query_group_width], projected_rows[:, :, query_group_width + 1], page_rows, prefix_counts, tail_pool, tail_len))
        attended = attended.reshape(REQUEST_COUNT, QUERY_HEADS * HEAD_DIMENSION)
        state = (state_f32 + jnp.dot(attended, weight_out, preferred_element_type=jnp.float32)).astype(jnp.bfloat16)
    return state
```

```python
import functools

import jax
import jax.numpy as jnp
from jax import lax
from jax.experimental import pallas as pl
from jax.experimental.pallas import tpu as pltpu
from jax.sharding import PartitionSpec as P

MODEL_WIDTH = 8192
LAYERS = 2
EPS = 1e-05
MESH = pl.DeviceIdType.MESH
D = 128
HEADS = 2
QH = 8
J = QH + 2
B = 8
KEYS = 1024
CHUNKS = ((0, 1, 2, 3), (4, 5, 6, 7, 8, 9))
MASKED = -1e30


def dot(a, b):
    return jnp.dot(a, b, preferred_element_type=jnp.float32)


def kernel(
    n_kv, n_req, pages, tail_span,
    hidden, gain, lim, tlen, w_hbm, wo_hbm, pre_hbm, tail_hbm,
    out,
    wbuf, wobuf, kvbuf, bias, scores, xe, qf, newkv, att,
    stall, ssall, part0, part1, ra0, ra1, sa0, sa1, rb0, rb1, attall, po, por,
    w_sem, kv_sem, wo_sem,
    st_s, st_r, ss_s, ss_r, ra_s, ra_r, rb_s, rb_r, at_s, at_r, fw_s, fw_r, po_s, po_r,
):
    kv = lax.axis_index("kv")
    req = lax.axis_index("req")
    core = lax.rem(req, 2)
    z = req // 2
    nz = n_req // 2
    sibling = (kv, z * 2 + 1 - core)
    rows, width = hidden.shape
    total_rows = n_kv * rows
    prefix_rows = pages * 128
    old_keys = prefix_rows + tail_span * B
    key_cols = 2 * old_keys
    parts, ras, sas, rbs = (part0, part1), (ra0, ra1), (sa0, sa1), (rb0, rb1)

    w_copies = [pltpu.make_async_copy(w_hbm.at[:, j], wbuf.at[j], w_sem.at[j]) for j in range(J)]
    kv_copies = []
    for l in range(LAYERS):
        row = []
        for s in range(2):
            row.append(pltpu.make_async_copy(
                pre_hbm.at[l, :, s], kvbuf.at[l, s, pl.ds(0, prefix_rows)], kv_sem.at[l, s, 0]))
            row.append(pltpu.make_async_copy(
                tail_hbm.at[l, :, s], kvbuf.at[l, s, pl.ds(prefix_rows, tail_span * B)], kv_sem.at[l, s, 1]))
        kv_copies.append(row)
    wo_copy = pltpu.make_async_copy(wo_hbm, wobuf, wo_sem)
    for c in w_copies:
        c.start()
    for c in kv_copies[0]:
        c.start()
    wo_copy.start()
    for c in kv_copies[1]:
        c.start()

    kv_peers = [(k, lax.rem(kv + k, n_kv)) for k in range(1, n_kv)]
    req_peers = [(k, lax.rem(req + k, n_req)) for k in range(1, n_req)]
    z_peers = [(k, lax.rem(z + k, nz)) for k in range(1, nz)]

    barrier = pltpu.get_barrier_semaphore()
    for _, p in kv_peers:
        pl.semaphore_signal(barrier, inc=1, device_id=(p, req), device_id_type=MESH)
    for _, p in req_peers:
        pl.semaphore_signal(barrier, inc=1, device_id=(kv, p), device_id_type=MESH)

    lane8 = lax.broadcasted_iota(jnp.int32, (B, 256), 1)
    limits = lim[...]
    for p in range(pages):
        ok = limits[:, p:p + 1] > lane8 // 2
        for c in range(HEADS):
            bias[c, :, p * 256:(p + 1) * 256] = jnp.where(ok & (lane8 % 2 == c), 0.0, MASKED)
    tails = tlen[...]
    lane = lax.broadcasted_iota(jnp.int32, (B, 2 * tail_span), 1)
    sub = lax.broadcasted_iota(jnp.int32, (B, 2 * tail_span), 0)
    for i in range(B):
        ok = (tails > lane // 2) & (sub == i)
        for c in range(HEADS):
            at = 2 * prefix_rows + i * 2 * tail_span
            bias[c, :, at:at + 2 * tail_span] = jnp.where(ok & (lane % 2 == c), 0.0, MASKED)
    lane1 = lax.broadcasted_iota(jnp.int32, (B, D), 1)
    sub1 = lax.broadcasted_iota(jnp.int32, (B, D), 0)
    for c in range(HEADS):
        bias[c, :, key_cols:key_cols + D] = jnp.where(lane1 == sub1 + c * B, 0.0, MASKED)
    newkv[...] = jnp.zeros_like(newkv)
    er = lax.broadcasted_iota(jnp.int32, (D, 4 * D), 0)
    ec = lax.broadcasted_iota(jnp.int32, (D, 4 * D), 1)
    expand = jnp.where(ec % 256 == 2 * er + ec // 256, 1.0, 0.0).astype(jnp.bfloat16)

    pl.semaphore_wait(barrier, (n_kv - 1) + (n_req - 1))

    sends = []

    def send(src, dst, ssem, rsem, dev):
        c = pltpu.make_async_remote_copy(
            src_ref=src, dst_ref=dst, send_sem=ssem, recv_sem=rsem, device_id=dev, device_id_type=MESH)
        c.start()
        sends.append(c)
        return c

    gains = gain[...].astype(jnp.float32)
    state = hidden[...]
    for l in range(LAYERS):
        stall[l, kv] = state
        copies = [send(stall.at[l, kv], stall.at[l, kv], st_s.at[l, k - 1], st_r.at[l, k - 1], (p, req))
                  for k, p in kv_peers]
        for c in copies:
            c.wait_recv()
        x = stall[l].reshape(total_rows, width).astype(jnp.float32)
        s = jnp.sum(x * x, axis=1, keepdims=True)
        packed = jnp.zeros((B, D), jnp.float32)
        for b in range(total_rows // B):
            packed = jnp.where(lane1 == b, s[b * B:(b + 1) * B], packed)
        ssall[l, req] = packed
        copies = [send(ssall.at[l, req], ssall.at[l, req], ss_s.at[l, k - 1], ss_r.at[l, k - 1], (kv, p))
                  for k, p in req_peers]
        for c in copies:
            c.wait_recv()
        tot = jnp.sum(ssall[l], axis=0)
        r = lax.rsqrt(tot / MODEL_WIDTH + EPS)
        scale = jnp.concatenate([r[:, b:b + 1] for b in range(total_rows // B)], axis=0)
        normed = (x * scale * gains).astype(jnp.bfloat16)
        for kb in range(width // D):
            e = dot(normed[:, kb * D:(kb + 1) * D], expand).astype(jnp.bfloat16)
            xe[0:total_rows, kb * 256:(kb + 1) * 256] = e[:, :256]
            xe[total_rows:, kb * 256:(kb + 1) * 256] = e[:, 256:]
        copies = []
        for ch, js in enumerate(CHUNKS):
            for a in range(0, len(js), 2):
                if l == 0:
                    w_copies[js[a]].wait()
                    w_copies[js[a + 1]].wait()
                w = jnp.concatenate([wbuf.at[js[a + t]].reshape(2 * width, D)[...] for t in range(2)], axis=1)
                y = dot(xe[...], w)
                for t in range(2):
                    for c in range(HEADS):
                        for b in range(n_req):
                            at = c * total_rows + b * B
                            parts[ch][l, b % 2, b // 2, a + t, c] = y[at:at + B, t * D:(t + 1) * D]
            copies.append(send(parts[ch].at[l, 1 - core], ras[ch].at[l], ra_s.at[l, ch], ra_r.at[l, ch], sibling))
        zc = []
        for ch, js in enumerate(CHUNKS):
            copies[ch].wait_recv()
            sas[ch][l] = parts[ch][l, core] + ras[ch][l]
            zc.append([send(sas[ch].at[l, p], rbs[ch].at[l, z], rb_s.at[l, ch, k - 1], rb_r.at[l, ch, k - 1],
                            (kv, p * 2 + core)) for k, p in z_peers])
            rbs[ch][l, z] = sas[ch][l, z]
        for ch, js in enumerate(CHUNKS):
            for c in zc[ch]:
                c.wait_recv()
            proj = jnp.sum(rbs[ch][l], axis=0)
            for t, j in enumerate(js):
                for c in range(HEADS):
                    if j < QH:
                        qf[(c * QH + j) * B:(c * QH + j + 1) * B] = proj[t, c]
                    else:
                        newkv[j - QH, c * B:(c + 1) * B] = proj[t, c]
        if l == 0:
            for c in kv_copies[0]:
                c.wait()
        else:
            for c in kv_copies[1]:
                c.wait()
        q = qf[...].astype(jnp.bfloat16)
        nq = HEADS * QH * B

        def score(k, at, span):
            raw = lax.dot_general(q, k, (((1,), (1,)), ((), ())), preferred_element_type=jnp.float32)
            raw = (raw * (D ** -0.5)).reshape(HEADS, QH, B, span) + bias[:, :, pl.ds(at, span)][:, None]
            raw = raw.reshape(nq, span)
            scores[:, pl.ds(at, span)] = raw
            top = raw[:, :D]
            for b in range(1, span // D):
                top = jnp.maximum(top, raw[:, b * D:(b + 1) * D])
            return top

        def score_step(step, top):
            k = kvbuf.at[l, 0, pl.ds(step * (KEYS // 2), KEYS // 2)].reshape(KEYS, D)[...]
            return jnp.maximum(top, score(k, pl.multiple_of(step * KEYS, KEYS), KEYS))

        top = score(newkv[0].astype(jnp.bfloat16), key_cols, D)
        top = lax.fori_loop(0, key_cols // KEYS, score_step, top)
        row_max = jnp.max(top, axis=1, keepdims=True)

        def mix(v, at, span):
            wt = jnp.exp(scores[:, pl.ds(at, span)] - row_max)
            add = wt[:, :D]
            for b in range(1, span // D):
                add = add + wt[:, b * D:(b + 1) * D]
            return dot(wt.astype(jnp.bfloat16), v), add

        def mix_step(step, carry):
            mixed, den = carry
            v = kvbuf.at[l, 1, pl.ds(step * (KEYS // 2), KEYS // 2)].reshape(KEYS, D)[...]
            m, d = mix(v, pl.multiple_of(step * KEYS, KEYS), KEYS)
            return mixed + m, den + d

        carry = mix(newkv[1].astype(jnp.bfloat16), key_cols, D)
        mixed, den = lax.fori_loop(0, key_cols // KEYS, mix_step, carry)
        ao = (mixed / jnp.sum(den, axis=1, keepdims=True))
        for h in range(HEADS * QH):
            attall[l, req, :, h * D:(h + 1) * D] = ao[h * B:(h + 1) * B].astype(jnp.bfloat16)
        own = attall.at[l, req]
        copies = [send(own, own, at_s.at[l, k - 1], at_r.at[l, k - 1], (kv, p * 2 + core)) for k, p in z_peers]
        fwd = [send(own, own, fw_s.at[l, 0], fw_r.at[l, 0], sibling)]
        for (k, _), c in zip(z_peers, copies):
            c.wait_recv()
            got = attall.at[l, lax.rem(z + nz - k, nz) * 2 + core]
            fwd.append(send(got, got, fw_s.at[l, k], fw_r.at[l, k], sibling))
        for c in fwd:
            c.wait_recv()
        if l == 0:
            wo_copy.wait()
        heads_rows = attall[l].reshape(total_rows, HEADS * QH * D)
        half = po.shape[-1]
        copies = []
        for ch in range(po.shape[1]):
            y = dot(heads_rows, wobuf[:, ch * half:(ch + 1) * half])
            po[l, ch] = y.reshape(n_kv, rows, half)
            copies.append([send(po.at[l, ch, p], por.at[l, ch, kv], po_s.at[l, ch, k - 1], po_r.at[l, ch, k - 1],
                                (p, req)) for k, p in kv_peers])
            por[l, ch, kv] = po[l, ch, kv]
        sums = []
        for ch in range(po.shape[1]):
            for c in copies[ch]:
                c.wait_recv()
            sums.append(jnp.sum(por[l, ch], axis=0))
        summed = jnp.concatenate(sums, axis=1) if len(sums) > 1 else sums[0]
        state = (state.astype(jnp.float32) + summed).astype(jnp.bfloat16)
    out[...] = state
    for c in sends:
        c.wait_send()


def shards(n_kv, n_req, hidden, norm_gain, query_key_value_matrix, output_matrix, prefix_cache, tail_cache,
           prefix_group, prefix_len, prefix_pages, tail_len):
    rows, width = hidden.shape
    layers, pages, page_tokens = prefix_cache.shape[:3]
    tail_span = tail_cache.shape[2]
    spans = prefix_len[:, None] - page_tokens * jnp.arange(prefix_pages.shape[1], dtype=jnp.int32)[None, :]
    hit = prefix_pages[:, :, None] == jnp.arange(pages, dtype=jnp.int32)[None, None, :]
    by_group = jnp.sum(jnp.where(hit, spans[:, :, None], 0), axis=1)
    mine = prefix_group[:, None] == jnp.arange(prefix_len.shape[0], dtype=jnp.int32)[None, :]
    lim = jnp.sum(jnp.where(mine[:, :, None], by_group[None], 0), axis=1)
    w = query_key_value_matrix.transpose(0, 2, 1, 3)
    wo = output_matrix.reshape(-1, output_matrix.shape[-1])
    pre = prefix_cache.reshape(layers, pages * page_tokens, 2, HEADS, D)
    tails = tail_cache.reshape(layers, -1, 2, HEADS, D)
    total_rows = rows * n_kv
    nz = n_req // 2
    old_keys = pages * page_tokens + tails.shape[1]
    key_cols = 2 * old_keys
    nch = len(CHUNKS)
    half = 512 if width > 512 else width
    f32, bf16, dma = jnp.float32, jnp.bfloat16, pltpu.SemaphoreType.DMA
    vm = pltpu.VMEM
    lens = [len(js) for js in CHUNKS]
    scratch = [
        vm((J, width, HEADS, D), bf16),
        vm(wo.shape, bf16),
        vm((layers, 2, old_keys, HEADS, D), bf16),
        vm((HEADS, B, key_cols + D), f32),
        vm((HEADS * QH * B, key_cols + D), f32),
        vm((HEADS * total_rows, HEADS * width), bf16),
        vm((HEADS * QH * B, D), f32),
        vm((2, D, D), f32),
        vm((B, D), f32),
        vm((layers, n_kv, rows, width), bf16),
        vm((layers, n_req, B, D), f32),
    ]
    scratch += [vm((layers, 2, nz, n, HEADS, B, D), f32) for n in lens]
    for _ in range(3):
        scratch += [vm((layers, nz, n, HEADS, B, D), f32) for n in lens]
    scratch += [
        vm((layers, n_req, B, HEADS * QH * D), bf16),
        vm((layers, width // half, n_kv, rows, half), f32),
        vm((layers, width // half, n_kv, rows, half), f32),
        dma((J,)), dma((layers, 2, 2)), dma,
        dma((layers, n_kv - 1)), dma((layers, n_kv - 1)),
        dma((layers, n_req - 1)), dma((layers, n_req - 1)),
        dma((layers, nch)), dma((layers, nch)),
        dma((layers, nch, nz - 1)), dma((layers, nch, nz - 1)),
        dma((layers, nz - 1)), dma((layers, nz - 1)),
        dma((layers, nz)), dma((layers, nz)),
        dma((layers, width // half, n_kv - 1)), dma((layers, width // half, n_kv - 1)),
    ]
    inside = pl.BlockSpec(memory_space=pltpu.VMEM)
    outside = pl.BlockSpec(memory_space=pl.ANY)
    return pl.pallas_call(
        functools.partial(kernel, n_kv, n_req, pages, tail_span),
        out_shape=jax.ShapeDtypeStruct(hidden.shape, hidden.dtype),
        in_specs=[inside] * 4 + [outside] * 4,
        out_specs=inside,
        scratch_shapes=scratch,
        compiler_params=pltpu.CompilerParams(
            collective_id=0, has_side_effects=True, vmem_limit_bytes=60 * 1024 * 1024),
    )(hidden, norm_gain.reshape(1, -1), lim, tail_len.reshape(-1, 1), w, wo, pre, tails)


def solution(mesh):
    return jax.shard_map(
        functools.partial(shards, mesh.shape["kv"], mesh.shape["req"]),
        mesh=mesh,
        in_specs=(
            P("kv", "req"),
            P("req"),
            P("req", "kv", None, None),
            P("kv", None, None, "req"),
            P(None, "req", None, None, "kv", None),
            P(None, "req", None, None, "kv", None),
            P("req"),
            P("req"),
            P("req", None),
            P("req"),
        ),
        out_specs=P("kv", "req"),
        check_vma=False,
    )
```

```python
import functools

import jax
import jax.numpy as jnp
from jax import lax
from jax.experimental import pallas as pl
from jax.experimental.pallas import tpu as pltpu
from jax.sharding import PartitionSpec as P

MODEL_WIDTH = 8192
LAYERS = 2
EPS = 1e-05
MESH = pl.DeviceIdType.MESH
D = 128
HEADS = 2
QH = 8
J = QH + 2
B = 8
KEYS = 1024
CHUNKS = ((8, 9, 0, 1), (2, 3), (4, 5, 6, 7))
GROUPS = ((0, 1), (2,))
GH = QH // len(GROUPS)
MASKED = -1e30


def dot(a, b):
    return jnp.dot(a, b, preferred_element_type=jnp.float32)


def kernel(
    n_kv, n_req, pages, tail_span,
    hidden, gain, group_of, prefix_len, page_at, tlen, w_hbm, wo_hbm, pre_hbm, tail_hbm,
    out,
    wbuf, wobuf, kvbuf, bias, scores, xe, qf, newkv,
    stall, ssall, totall, part0, part1, part2, ra0, ra1, ra2, sa0, sa1, sa2, rb0, rb1, rb2, attall, po, por,
    w_sem, kv_sem, wo_sem,
    st_s, st_r, ss_s, ss_r, to_s, to_r, ra_s, ra_r, rb_s, rb_r, at_s, at_r, po_s, po_r,
):
    kv = lax.axis_index("kv")
    req = lax.axis_index("req")
    core = lax.rem(req, 2)
    z = req // 2
    nz = n_req // 2
    sibling = (kv, z * 2 + 1 - core)
    rows, width = hidden.shape
    total_rows = n_kv * rows
    prefix_rows = pages * 128
    old_keys = prefix_rows + tail_span * B
    key_cols = 2 * old_keys
    parts, ras, sas, rbs = (part0, part1, part2), (ra0, ra1, ra2), (sa0, sa1, sa2), (rb0, rb1, rb2)

    w_copies = [pltpu.make_async_copy(w_hbm.at[:, j], wbuf.at[j], w_sem.at[j]) for j in range(J)]
    kv_copies = []
    for l in range(LAYERS):
        row = []
        for s in range(2):
            row.append(pltpu.make_async_copy(
                pre_hbm.at[l, :, s], kvbuf.at[l, s, pl.ds(0, prefix_rows)], kv_sem.at[l, s, 0]))
            row.append(pltpu.make_async_copy(
                tail_hbm.at[l, :, s], kvbuf.at[l, s, pl.ds(prefix_rows, tail_span * B)], kv_sem.at[l, s, 1]))
        kv_copies.append(row)
    wo_copy = pltpu.make_async_copy(wo_hbm, wobuf, wo_sem)
    for c in w_copies:
        c.start()
    for c in kv_copies[0]:
        c.start()
    wo_copy.start()
    for c in kv_copies[1]:
        c.start()

    kv_peers = [(k, lax.rem(kv + k, n_kv)) for k in range(1, n_kv)]
    req_peers = [(k, lax.rem(req + k, n_req)) for k in range(1, n_req)]
    z_peers = [(k, lax.rem(z + k, nz)) for k in range(1, nz)]

    barrier = pltpu.get_barrier_semaphore()
    for _, p in kv_peers:
        pl.semaphore_signal(barrier, inc=1, device_id=(p, req), device_id_type=MESH)
    for _, p in req_peers:
        pl.semaphore_signal(barrier, inc=1, device_id=(kv, p), device_id_type=MESH)

    lane1 = lax.broadcasted_iota(jnp.int32, (B, D), 1)
    sub1 = lax.broadcasted_iota(jnp.int32, (B, D), 0)

    def masks():
        by_group = []
        for g in range(page_at.shape[0]):
            row = jnp.zeros((B, D), jnp.int32)
            for t in range(page_at.shape[1]):
                row = jnp.where(lane1 == page_at[g, t], prefix_len[g] - 128 * t, row)
            by_group.append(row)
        limits = jnp.zeros((B, D), jnp.int32)
        for i in range(B):
            for g in range(page_at.shape[0]):
                limits = jnp.where((sub1 == i) & (group_of[i] == g), by_group[g], limits)
        lane8 = lax.broadcasted_iota(jnp.int32, (B, 256), 1)
        for p in range(pages):
            ok = limits[:, p:p + 1] > lane8 // 2
            for c in range(HEADS):
                bias[c, :, p * 256:(p + 1) * 256] = jnp.where(ok & (lane8 % 2 == c), 0.0, MASKED)
        lane = lax.broadcasted_iota(jnp.int32, (B, 2 * tail_span), 1)
        sub = lax.broadcasted_iota(jnp.int32, (B, 2 * tail_span), 0)
        for i in range(B):
            ok = (lane // 2 < tlen[i]) & (sub == i)
            for c in range(HEADS):
                at = 2 * prefix_rows + i * 2 * tail_span
                bias[c, :, at:at + 2 * tail_span] = jnp.where(ok & (lane % 2 == c), 0.0, MASKED)
        for c in range(HEADS):
            bias[c, :, key_cols:key_cols + D] = jnp.where(lane1 == sub1 + c * B, 0.0, MASKED)
        newkv[...] = jnp.zeros_like(newkv)

    er = lax.broadcasted_iota(jnp.int32, (D, 4 * D), 0)
    ec = lax.broadcasted_iota(jnp.int32, (D, 4 * D), 1)
    expand = jnp.where(ec % 256 == 2 * er + ec // 256, 1.0, 0.0).astype(jnp.bfloat16)

    pl.semaphore_wait(barrier, (n_kv - 1) + (n_req - 1))

    sends = []

    def send(src, dst, ssem, rsem, dev):
        c = pltpu.make_async_remote_copy(
            src_ref=src, dst_ref=dst, send_sem=ssem, recv_sem=rsem, device_id=dev, device_id_type=MESH)
        c.start()
        sends.append(c)
        return c

    def attend(l, q, nq):
        def score(k, at, span):
            raw = lax.dot_general(q, k, (((1,), (1,)), ((), ())), preferred_element_type=jnp.float32)
            raw = (raw * (D ** -0.5)).reshape(HEADS, GH, B, span) + bias[:, :, pl.ds(at, span)][:, None]
            raw = raw.reshape(nq, span)
            scores[:, pl.ds(at, span)] = raw
            top = raw[:, :D]
            for b in range(1, span // D):
                top = jnp.maximum(top, raw[:, b * D:(b + 1) * D])
            return top

        def score_step(step, top):
            k = kvbuf.at[l, 0, pl.ds(step * (KEYS // 2), KEYS // 2)].reshape(KEYS, D)[...]
            return jnp.maximum(top, score(k, pl.multiple_of(step * KEYS, KEYS), KEYS))

        top = score(newkv[0].astype(jnp.bfloat16), key_cols, D)
        top = lax.fori_loop(0, key_cols // KEYS, score_step, top)
        row_max = jnp.max(top, axis=1, keepdims=True)

        def mix(v, at, span):
            wt = jnp.exp(scores[:, pl.ds(at, span)] - row_max)
            add = wt[:, :D]
            for b in range(1, span // D):
                add = add + wt[:, b * D:(b + 1) * D]
            return dot(wt.astype(jnp.bfloat16), v), add

        def mix_step(step, carry):
            mixed, den = carry
            v = kvbuf.at[l, 1, pl.ds(step * (KEYS // 2), KEYS // 2)].reshape(KEYS, D)[...]
            m, d = mix(v, pl.multiple_of(step * KEYS, KEYS), KEYS)
            return mixed + m, den + d

        carry = mix(newkv[1].astype(jnp.bfloat16), key_cols, D)
        mixed, den = lax.fori_loop(0, key_cols // KEYS, mix_step, carry)
        return mixed / jnp.sum(den, axis=1, keepdims=True)

    gains = gain[...].astype(jnp.float32).reshape(1, width)
    state = hidden[...]
    for l in range(LAYERS):
        stall[l, kv] = state
        st_copies = [send(stall.at[l, kv], stall.at[l, kv], st_s.at[l, k - 1], st_r.at[l, k - 1], (p, req))
                     for k, p in kv_peers]
        own = state.astype(jnp.float32)
        s = jnp.sum(own * own, axis=1, keepdims=True)
        packed = jnp.zeros((B, D), jnp.float32)
        for b in range(rows // B):
            packed = jnp.where(lane1 == b, s[b * B:(b + 1) * B], packed)
        ssall[l, req] = packed
        copies = [send(ssall.at[l, req], ssall.at[l, req], ss_s.at[l, k - 1], ss_r.at[l, k - 1], (kv, p))
                  for k, p in req_peers]
        if l == 0:
            masks()
        for c in copies:
            c.wait_recv()
        totall[l, kv] = jnp.sum(ssall[l], axis=0)
        copies = [send(totall.at[l, kv], totall.at[l, kv], to_s.at[l, k - 1], to_r.at[l, k - 1], (p, req))
                  for k, p in kv_peers]
        for c in st_copies:
            c.wait_recv()
        x = stall[l].reshape(total_rows, width).astype(jnp.float32)
        for c in copies:
            c.wait_recv()
        r = lax.rsqrt(totall[l] / MODEL_WIDTH + EPS)
        scale = jnp.concatenate([r[m, :, b:b + 1] for m in range(n_kv) for b in range(rows // B)], axis=0)
        normed = (x * scale * gains).astype(jnp.bfloat16)
        for kb in range(width // D):
            e = dot(normed[:, kb * D:(kb + 1) * D], expand).astype(jnp.bfloat16)
            xe[0:total_rows, kb * 256:(kb + 1) * 256] = e[:, :256]
            xe[total_rows:, kb * 256:(kb + 1) * 256] = e[:, 256:]
        copies, zc = [], []

        def pass_on(ch):
            copies[ch].wait_recv()
            sas[ch][l] = parts[ch][l, core] + ras[ch][l]
            zc.append([send(sas[ch].at[l, p], rbs[ch].at[l, z], rb_s.at[l, ch, k - 1], rb_r.at[l, ch, k - 1],
                            (kv, p * 2 + core)) for k, p in z_peers])
            rbs[ch][l, z] = sas[ch][l, z]

        for ch, js in enumerate(CHUNKS):
            for a in range(0, len(js), 2):
                if l == 0:
                    w_copies[js[a]].wait()
                    w_copies[js[a + 1]].wait()
                w = jnp.concatenate([wbuf.at[js[a + t]].reshape(2 * width, D)[...] for t in range(2)], axis=1)
                y = dot(xe[...], w)
                for t in range(2):
                    for c in range(HEADS):
                        for b in range(n_req):
                            at = c * total_rows + b * B
                            parts[ch][l, b % 2, b // 2, a + t, c] = y[at:at + B, t * D:(t + 1) * D]
            copies.append(send(parts[ch].at[l, 1 - core], ras[ch].at[l], ra_s.at[l, ch], ra_r.at[l, ch], sibling))
            if ch >= 1:
                pass_on(ch - 1)
        pass_on(len(CHUNKS) - 1)
        nq = HEADS * GH * B
        at_copies = []
        for g, members in enumerate(GROUPS):
            for ch in members:
                for c in zc[ch]:
                    c.wait_recv()
                proj = jnp.sum(rbs[ch][l], axis=0)
                for t, j in enumerate(CHUNKS[ch]):
                    for c in range(HEADS):
                        if j < QH:
                            at = (c * GH + j % GH) * B
                            qf[g, at:at + B] = proj[t, c]
                        else:
                            newkv[j - QH, c * B:(c + 1) * B] = proj[t, c]
            if g == 0:
                for c in kv_copies[l]:
                    c.wait()
            ao = attend(l, qf[g].astype(jnp.bfloat16), nq)
            for h in range(HEADS * GH):
                attall[l, g, req, :, h * D:(h + 1) * D] = ao[h * B:(h + 1) * B].astype(jnp.bfloat16)
            own_rows = attall.at[l, g, req]
            at_copies.append([send(own_rows, own_rows, at_s.at[l, g, k - 1], at_r.at[l, g, k - 1], (kv, p))
                              for k, p in req_peers])
        if l == 0:
            wo_copy.wait()
        half = po.shape[-1]
        slices = po.shape[1]
        span = GH * D
        sums = [None] * slices
        copies = []
        for g in range(len(GROUPS)):
            for c in at_copies[g]:
                c.wait_recv()
            heads_rows = attall[l, g].reshape(total_rows, HEADS * span)
            for ch in range(slices):
                y = sums[ch]
                for c in range(HEADS):
                    at = (c * QH + g * GH) * D
                    part = dot(heads_rows[:, c * span:(c + 1) * span], wobuf[at:at + span, ch * half:(ch + 1) * half])
                    y = part if y is None else y + part
                sums[ch] = y
                if g == len(GROUPS) - 1:
                    po[l, ch] = y.reshape(n_kv, rows, half)
                    copies.append([send(po.at[l, ch, p], por.at[l, ch, kv], po_s.at[l, ch, k - 1],
                                        po_r.at[l, ch, k - 1], (p, req)) for k, p in kv_peers])
                    por[l, ch, kv] = po[l, ch, kv]
        sums = []
        for ch in range(po.shape[1]):
            for c in copies[ch]:
                c.wait_recv()
            sums.append(jnp.sum(por[l, ch], axis=0))
        summed = jnp.concatenate(sums, axis=1) if len(sums) > 1 else sums[0]
        state = (state.astype(jnp.float32) + summed).astype(jnp.bfloat16)
    out[...] = state
    for c in sends:
        c.wait_send()


def shards(n_kv, n_req, hidden, norm_gain, query_key_value_matrix, output_matrix, prefix_cache, tail_cache,
           prefix_group, prefix_len, prefix_pages, tail_len):
    rows, width = hidden.shape
    layers, pages, page_tokens = prefix_cache.shape[:3]
    tail_span = tail_cache.shape[2]
    w = query_key_value_matrix.transpose(0, 2, 1, 3)
    wo = output_matrix.reshape(-1, output_matrix.shape[-1])
    pre = prefix_cache.reshape(layers, pages * page_tokens, 2, HEADS, D)
    tails = tail_cache.reshape(layers, -1, 2, HEADS, D)
    total_rows = rows * n_kv
    nz = n_req // 2
    old_keys = pages * page_tokens + tails.shape[1]
    key_cols = 2 * old_keys
    nch = len(CHUNKS)
    half = 512 if width > 512 else width
    f32, bf16, dma = jnp.float32, jnp.bfloat16, pltpu.SemaphoreType.DMA
    vm = pltpu.VMEM
    lens = [len(js) for js in CHUNKS]
    scratch = [
        vm((J, width, HEADS, D), bf16),
        vm(wo.shape, bf16),
        vm((layers, 2, old_keys, HEADS, D), bf16),
        vm((HEADS, B, key_cols + D), f32),
        vm((HEADS * GH * B, key_cols + D), f32),
        vm((HEADS * total_rows, HEADS * width), bf16),
        vm((len(GROUPS), HEADS * GH * B, D), f32),
        vm((2, D, D), f32),
        vm((layers, n_kv, rows, width), bf16),
        vm((layers, n_req, B, D), f32),
        vm((layers, n_kv, B, D), f32),
    ]
    scratch += [vm((layers, 2, nz, n, HEADS, B, D), f32) for n in lens]
    for _ in range(3):
        scratch += [vm((layers, nz, n, HEADS, B, D), f32) for n in lens]
    scratch += [
        vm((layers, len(GROUPS), n_req, B, HEADS * GH * D), bf16),
        vm((layers, width // half, n_kv, rows, half), f32),
        vm((layers, width // half, n_kv, rows, half), f32),
        dma((J,)), dma((layers, 2, 2)), dma,
        dma((layers, n_kv - 1)), dma((layers, n_kv - 1)),
        dma((layers, n_req - 1)), dma((layers, n_req - 1)),
        dma((layers, n_kv - 1)), dma((layers, n_kv - 1)),
        dma((layers, nch)), dma((layers, nch)),
        dma((layers, nch, nz - 1)), dma((layers, nch, nz - 1)),
        dma((layers, len(GROUPS), n_req - 1)), dma((layers, len(GROUPS), n_req - 1)),
        dma((layers, width // half, n_kv - 1)), dma((layers, width // half, n_kv - 1)),
    ]
    inside = pl.BlockSpec(memory_space=pltpu.VMEM)
    scalars = pl.BlockSpec(memory_space=pltpu.SMEM)
    outside = pl.BlockSpec(memory_space=pl.ANY)
    return pl.pallas_call(
        functools.partial(kernel, n_kv, n_req, pages, tail_span),
        out_shape=jax.ShapeDtypeStruct(hidden.shape, hidden.dtype),
        in_specs=[inside] * 2 + [scalars] * 4 + [outside] * 4,
        out_specs=inside,
        scratch_shapes=scratch,
        compiler_params=pltpu.CompilerParams(
            collective_id=0, has_side_effects=True, vmem_limit_bytes=60 * 1024 * 1024),
    )(hidden, norm_gain, prefix_group, prefix_len, prefix_pages, tail_len, w, wo, pre, tails)


def solution(mesh):
    return jax.shard_map(
        functools.partial(shards, mesh.shape["kv"], mesh.shape["req"]),
        mesh=mesh,
        in_specs=(
            P("kv", "req"),
            P("req"),
            P("req", "kv", None, None),
            P("kv", None, None, "req"),
            P(None, "req", None, None, "kv", None),
            P(None, "req", None, None, "kv", None),
            P("req"),
            P("req"),
            P("req", None),
            P("req"),
        ),
        out_specs=P("kv", "req"),
        check_vma=False,
    )
```

```python
import functools

import jax
import jax.numpy as jnp
from jax import lax
from jax.experimental import pallas as pl
from jax.experimental.pallas import tpu as pltpu
from jax.sharding import PartitionSpec as P

MODEL_WIDTH = 8192
LAYERS = 2
EPS = 1e-05
MESH = pl.DeviceIdType.MESH
D = 128
HEADS = 2
QH = 8
J = QH + 2
B = 8
KEYS = 1024
CHUNKS = ((8, 9, 0, 1), (2, 3), (4, 5, 6, 7))
GROUPS = ((0, 1, 2),)
GH = QH // len(GROUPS)
MASKED = -1e30


def dot(a, b):
    return jnp.dot(a, b, preferred_element_type=jnp.float32)


def kernel(
    n_kv, n_req, pages, tail_span,
    hidden, gain, group_of, prefix_len, page_at, tlen, w_hbm, wo_hbm, pre_hbm, tail_hbm,
    out,
    wbuf, wobuf, kvbuf, bias, scores, xe, qf, newkv,
    stall, ssall, totall, part0, part1, part2, ra0, ra1, ra2, sa0, sa1, sa2, rb0, rb1, rb2, attall, po, por,
    w_sem, kv_sem, wo_sem,
    st_s, st_r, ss_s, ss_r, to_s, to_r, ra_s, ra_r, rb_s, rb_r, at_s, at_r, po_s, po_r,
):
    kv = lax.axis_index("kv")
    req = lax.axis_index("req")
    core = lax.rem(req, 2)
    z = req // 2
    nz = n_req // 2
    sibling = (kv, z * 2 + 1 - core)
    rows, width = hidden.shape
    total_rows = n_kv * rows
    prefix_rows = pages * 128
    old_keys = prefix_rows + tail_span * B
    key_cols = 2 * old_keys
    parts, ras, sas, rbs = (part0, part1, part2), (ra0, ra1, ra2), (sa0, sa1, sa2), (rb0, rb1, rb2)

    w_copies = [pltpu.make_async_copy(w_hbm.at[:, j], wbuf.at[j], w_sem.at[j]) for j in range(J)]
    kv_copies = []
    for l in range(LAYERS):
        row = []
        for s in range(2):
            row.append(pltpu.make_async_copy(
                pre_hbm.at[l, :, s], kvbuf.at[l, s, pl.ds(0, prefix_rows)], kv_sem.at[l, s, 0]))
            row.append(pltpu.make_async_copy(
                tail_hbm.at[l, :, s], kvbuf.at[l, s, pl.ds(prefix_rows, tail_span * B)], kv_sem.at[l, s, 1]))
        kv_copies.append(row)
    wo_copy = pltpu.make_async_copy(wo_hbm, wobuf, wo_sem)
    for c in w_copies:
        c.start()
    for c in kv_copies[0]:
        c.start()
    wo_copy.start()
    for c in kv_copies[1]:
        c.start()

    kv_peers = [(k, lax.rem(kv + k, n_kv)) for k in range(1, n_kv)]
    req_peers = [(k, lax.rem(req + k, n_req)) for k in range(1, n_req)]
    z_peers = [(k, lax.rem(z + k, nz)) for k in range(1, nz)]

    barrier = pltpu.get_barrier_semaphore()
    for _, p in kv_peers:
        pl.semaphore_signal(barrier, inc=1, device_id=(p, req), device_id_type=MESH)
    for _, p in req_peers:
        pl.semaphore_signal(barrier, inc=1, device_id=(kv, p), device_id_type=MESH)

    lane1 = lax.broadcasted_iota(jnp.int32, (B, D), 1)
    sub1 = lax.broadcasted_iota(jnp.int32, (B, D), 0)

    def masks():
        by_group = []
        for g in range(page_at.shape[0]):
            row = jnp.zeros((B, D), jnp.int32)
            for t in range(page_at.shape[1]):
                row = jnp.where(lane1 == page_at[g, t], prefix_len[g] - 128 * t, row)
            by_group.append(row)
        limits = jnp.zeros((B, D), jnp.int32)
        for i in range(B):
            for g in range(page_at.shape[0]):
                limits = jnp.where((sub1 == i) & (group_of[i] == g), by_group[g], limits)
        lane8 = lax.broadcasted_iota(jnp.int32, (B, 256), 1)
        for p in range(pages):
            ok = limits[:, p:p + 1] > lane8 // 2
            for c in range(HEADS):
                bias[c, :, p * 256:(p + 1) * 256] = jnp.where(ok & (lane8 % 2 == c), 0.0, MASKED)
        lane = lax.broadcasted_iota(jnp.int32, (B, 2 * tail_span), 1)
        sub = lax.broadcasted_iota(jnp.int32, (B, 2 * tail_span), 0)
        for i in range(B):
            ok = (lane // 2 < tlen[i]) & (sub == i)
            for c in range(HEADS):
                at = 2 * prefix_rows + i * 2 * tail_span
                bias[c, :, at:at + 2 * tail_span] = jnp.where(ok & (lane % 2 == c), 0.0, MASKED)
        for c in range(HEADS):
            bias[c, :, key_cols:key_cols + D] = jnp.where(lane1 == sub1 + c * B, 0.0, MASKED)
        newkv[...] = jnp.zeros_like(newkv)

    er = lax.broadcasted_iota(jnp.int32, (D, 4 * D), 0)
    ec = lax.broadcasted_iota(jnp.int32, (D, 4 * D), 1)
    expand = jnp.where(ec % 256 == 2 * er + ec // 256, 1.0, 0.0).astype(jnp.bfloat16)

    pl.semaphore_wait(barrier, (n_kv - 1) + (n_req - 1))

    sends = []

    def send(src, dst, ssem, rsem, dev):
        c = pltpu.make_async_remote_copy(
            src_ref=src, dst_ref=dst, send_sem=ssem, recv_sem=rsem, device_id=dev, device_id_type=MESH)
        c.start()
        sends.append(c)
        return c

    def attend(l, q, nq):
        def score(k, at, span):
            raw = lax.dot_general(q, k, (((1,), (1,)), ((), ())), preferred_element_type=jnp.float32)
            raw = (raw * (D ** -0.5)).reshape(HEADS, GH, B, span) + bias[:, :, pl.ds(at, span)][:, None]
            raw = raw.reshape(nq, span)
            scores[:, pl.ds(at, span)] = raw
            top = raw[:, :D]
            for b in range(1, span // D):
                top = jnp.maximum(top, raw[:, b * D:(b + 1) * D])
            return top

        def score_step(step, top):
            k = kvbuf.at[l, 0, pl.ds(step * (KEYS // 2), KEYS // 2)].reshape(KEYS, D)[...]
            return jnp.maximum(top, score(k, pl.multiple_of(step * KEYS, KEYS), KEYS))

        top = score(newkv[0].astype(jnp.bfloat16), key_cols, D)
        top = lax.fori_loop(0, key_cols // KEYS, score_step, top)
        row_max = jnp.max(top, axis=1, keepdims=True)

        def mix(v, at, span):
            wt = jnp.exp(scores[:, pl.ds(at, span)] - row_max)
            add = wt[:, :D]
            for b in range(1, span // D):
                add = add + wt[:, b * D:(b + 1) * D]
            return dot(wt.astype(jnp.bfloat16), v), add

        def mix_step(step, carry):
            mixed, den = carry
            v = kvbuf.at[l, 1, pl.ds(step * (KEYS // 2), KEYS // 2)].reshape(KEYS, D)[...]
            m, d = mix(v, pl.multiple_of(step * KEYS, KEYS), KEYS)
            return mixed + m, den + d

        carry = mix(newkv[1].astype(jnp.bfloat16), key_cols, D)
        mixed, den = lax.fori_loop(0, key_cols // KEYS, mix_step, carry)
        return mixed / jnp.sum(den, axis=1, keepdims=True)

    gains = gain[...].astype(jnp.float32).reshape(1, width)
    state = hidden[...]
    for l in range(LAYERS):
        stall[l, kv] = state
        st_copies = [send(stall.at[l, kv], stall.at[l, kv], st_s.at[l, k - 1], st_r.at[l, k - 1], (p, req))
                     for k, p in kv_peers]
        own = state.astype(jnp.float32)
        s = jnp.sum(own * own, axis=1, keepdims=True)
        packed = jnp.zeros((B, D), jnp.float32)
        for b in range(rows // B):
            packed = jnp.where(lane1 == b, s[b * B:(b + 1) * B], packed)
        ssall[l, req] = packed
        copies = [send(ssall.at[l, req], ssall.at[l, req], ss_s.at[l, k - 1], ss_r.at[l, k - 1], (kv, p))
                  for k, p in req_peers]
        if l == 0:
            masks()
        for c in copies:
            c.wait_recv()
        totall[l, kv] = jnp.sum(ssall[l], axis=0)
        copies = [send(totall.at[l, kv], totall.at[l, kv], to_s.at[l, k - 1], to_r.at[l, k - 1], (p, req))
                  for k, p in kv_peers]
        for c in st_copies:
            c.wait_recv()
        x = stall[l].reshape(total_rows, width).astype(jnp.float32)
        for c in copies:
            c.wait_recv()
        r = lax.rsqrt(totall[l] / MODEL_WIDTH + EPS)
        scale = jnp.concatenate([r[m, :, b:b + 1] for m in range(n_kv) for b in range(rows // B)], axis=0)
        normed = (x * scale * gains).astype(jnp.bfloat16)
        for kb in range(width // D):
            e = dot(normed[:, kb * D:(kb + 1) * D], expand).astype(jnp.bfloat16)
            xe[0:total_rows, kb * 256:(kb + 1) * 256] = e[:, :256]
            xe[total_rows:, kb * 256:(kb + 1) * 256] = e[:, 256:]
        copies, zc = [], []

        def pass_on(ch):
            copies[ch].wait_recv()
            sas[ch][l] = parts[ch][l, core] + ras[ch][l]
            zc.append([send(sas[ch].at[l, p], rbs[ch].at[l, z], rb_s.at[l, ch, k - 1], rb_r.at[l, ch, k - 1],
                            (kv, p * 2 + core)) for k, p in z_peers])
            rbs[ch][l, z] = sas[ch][l, z]

        for ch, js in enumerate(CHUNKS):
            for a in range(0, len(js), 2):
                if l == 0:
                    w_copies[js[a]].wait()
                    w_copies[js[a + 1]].wait()
                w = jnp.concatenate([wbuf.at[js[a + t]].reshape(2 * width, D)[...] for t in range(2)], axis=1)
                y = dot(xe[...], w)
                for t in range(2):
                    for c in range(HEADS):
                        for b in range(n_req):
                            at = c * total_rows + b * B
                            parts[ch][l, b % 2, b // 2, a + t, c] = y[at:at + B, t * D:(t + 1) * D]
            copies.append(send(parts[ch].at[l, 1 - core], ras[ch].at[l], ra_s.at[l, ch], ra_r.at[l, ch], sibling))
            if ch >= 1:
                pass_on(ch - 1)
        pass_on(len(CHUNKS) - 1)
        nq = HEADS * GH * B
        at_copies = []
        for g, members in enumerate(GROUPS):
            for ch in members:
                for c in zc[ch]:
                    c.wait_recv()
                proj = jnp.sum(rbs[ch][l], axis=0)
                for t, j in enumerate(CHUNKS[ch]):
                    for c in range(HEADS):
                        if j < QH:
                            at = (c * GH + j % GH) * B
                            qf[g, at:at + B] = proj[t, c]
                        else:
                            newkv[j - QH, c * B:(c + 1) * B] = proj[t, c]
            if g == 0:
                for c in kv_copies[l]:
                    c.wait()
            ao = attend(l, qf[g].astype(jnp.bfloat16), nq)
            for h in range(HEADS * GH):
                attall[l, g, req, :, h * D:(h + 1) * D] = ao[h * B:(h + 1) * B].astype(jnp.bfloat16)
            own_rows = attall.at[l, g, req]
            z_copies = [send(own_rows, own_rows, at_s.at[l, g, k - 1], at_r.at[l, g, k - 1], (kv, p * 2 + core))
                        for k, p in z_peers]
            fwd = [send(own_rows, own_rows, at_s.at[l, g, nz - 1], at_r.at[l, g, nz - 1], sibling)]
            for (k, _), c in zip(z_peers, z_copies):
                c.wait_recv()
                got = attall.at[l, g, lax.rem(z + nz - k, nz) * 2 + core]
                fwd.append(send(got, got, at_s.at[l, g, nz - 1 + k], at_r.at[l, g, nz - 1 + k], sibling))
            at_copies.append(fwd)
        if l == 0:
            wo_copy.wait()
        half = po.shape[-1]
        slices = po.shape[1]
        span = GH * D
        sums = [None] * slices
        copies = []
        for g in range(len(GROUPS)):
            for c in at_copies[g]:
                c.wait_recv()
            heads_rows = attall[l, g].reshape(total_rows, HEADS * span)
            for ch in range(slices):
                y = sums[ch]
                for c in range(HEADS):
                    at = (c * QH + g * GH) * D
                    part = dot(heads_rows[:, c * span:(c + 1) * span], wobuf[at:at + span, ch * half:(ch + 1) * half])
                    y = part if y is None else y + part
                sums[ch] = y
                if g == len(GROUPS) - 1:
                    po[l, ch] = y.reshape(n_kv, rows, half)
                    copies.append([send(po.at[l, ch, p], por.at[l, ch, kv], po_s.at[l, ch, k - 1],
                                        po_r.at[l, ch, k - 1], (p, req)) for k, p in kv_peers])
                    por[l, ch, kv] = po[l, ch, kv]
        sums = []
        for ch in range(po.shape[1]):
            for c in copies[ch]:
                c.wait_recv()
            sums.append(jnp.sum(por[l, ch], axis=0))
        summed = jnp.concatenate(sums, axis=1) if len(sums) > 1 else sums[0]
        state = (state.astype(jnp.float32) + summed).astype(jnp.bfloat16)
    out[...] = state
    for c in sends:
        c.wait_send()


def shards(n_kv, n_req, hidden, norm_gain, query_key_value_matrix, output_matrix, prefix_cache, tail_cache,
           prefix_group, prefix_len, prefix_pages, tail_len):
    rows, width = hidden.shape
    layers, pages, page_tokens = prefix_cache.shape[:3]
    tail_span = tail_cache.shape[2]
    w = query_key_value_matrix.transpose(0, 2, 1, 3)
    wo = output_matrix.reshape(-1, output_matrix.shape[-1])
    pre = prefix_cache.reshape(layers, pages * page_tokens, 2, HEADS, D)
    tails = tail_cache.reshape(layers, -1, 2, HEADS, D)
    total_rows = rows * n_kv
    nz = n_req // 2
    old_keys = pages * page_tokens + tails.shape[1]
    key_cols = 2 * old_keys
    nch = len(CHUNKS)
    half = 512 if width > 512 else width
    f32, bf16, dma = jnp.float32, jnp.bfloat16, pltpu.SemaphoreType.DMA
    vm = pltpu.VMEM
    lens = [len(js) for js in CHUNKS]
    scratch = [
        vm((J, width, HEADS, D), bf16),
        vm(wo.shape, bf16),
        vm((layers, 2, old_keys, HEADS, D), bf16),
        vm((HEADS, B, key_cols + D), f32),
        vm((HEADS * GH * B, key_cols + D), f32),
        vm((HEADS * total_rows, HEADS * width), bf16),
        vm((len(GROUPS), HEADS * GH * B, D), f32),
        vm((2, D, D), f32),
        vm((layers, n_kv, rows, width), bf16),
        vm((layers, n_req, B, D), f32),
        vm((layers, n_kv, B, D), f32),
    ]
    scratch += [vm((layers, 2, nz, n, HEADS, B, D), f32) for n in lens]
    for _ in range(3):
        scratch += [vm((layers, nz, n, HEADS, B, D), f32) for n in lens]
    scratch += [
        vm((layers, len(GROUPS), n_req, B, HEADS * GH * D), bf16),
        vm((layers, width // half, n_kv, rows, half), f32),
        vm((layers, width // half, n_kv, rows, half), f32),
        dma((J,)), dma((layers, 2, 2)), dma,
        dma((layers, n_kv - 1)), dma((layers, n_kv - 1)),
        dma((layers, n_req - 1)), dma((layers, n_req - 1)),
        dma((layers, n_kv - 1)), dma((layers, n_kv - 1)),
        dma((layers, nch)), dma((layers, nch)),
        dma((layers, nch, nz - 1)), dma((layers, nch, nz - 1)),
        dma((layers, len(GROUPS), n_req - 1)), dma((layers, len(GROUPS), n_req - 1)),
        dma((layers, width // half, n_kv - 1)), dma((layers, width // half, n_kv - 1)),
    ]
    inside = pl.BlockSpec(memory_space=pltpu.VMEM)
    scalars = pl.BlockSpec(memory_space=pltpu.SMEM)
    outside = pl.BlockSpec(memory_space=pl.ANY)
    return pl.pallas_call(
        functools.partial(kernel, n_kv, n_req, pages, tail_span),
        out_shape=jax.ShapeDtypeStruct(hidden.shape, hidden.dtype),
        in_specs=[inside] * 2 + [scalars] * 4 + [outside] * 4,
        out_specs=inside,
        scratch_shapes=scratch,
        compiler_params=pltpu.CompilerParams(
            collective_id=0, has_side_effects=True, vmem_limit_bytes=60 * 1024 * 1024),
    )(hidden, norm_gain, prefix_group, prefix_len, prefix_pages, tail_len, w, wo, pre, tails)


def solution(mesh):
    return jax.shard_map(
        functools.partial(shards, mesh.shape["kv"], mesh.shape["req"]),
        mesh=mesh,
        in_specs=(
            P("kv", "req"),
            P("req"),
            P("req", "kv", None, None),
            P("kv", None, None, "req"),
            P(None, "req", None, None, "kv", None),
            P(None, "req", None, None, "kv", None),
            P("req"),
            P("req"),
            P("req", None),
            P("req"),
        ),
        out_specs=P("kv", "req"),
        check_vma=False,
    )
```
